512 devices in a mesh: ctx: 64 (over x, y, z_hi, core), head: 8 (over z_lo).
Axes of the slice: x: 4, y: 4, z: 16 (z_hi: 2, z_lo: 8; z = z_hi * 8 + z_lo), core: 2. Of those that a mesh axis runs over, the one named last changes fastest.
Arguments:
- queries: bfloat16 [16384, 32, 128], P('ctx', 'head'), may hold values from -300 to 300
- keys: bfloat16 [16384, 8, 128], P('ctx', 'head'), may hold values from -12 to 12
- values: bfloat16 [16384, 8, 128], P('ctx', 'head'), may hold values from -150 to 150
- tangent_queries: bfloat16 [16384, 32, 128], P('ctx', 'head'), may hold values from -6 to 6
- tangent_keys: bfloat16 [16384, 8, 128], P('ctx', 'head'), may hold values from -6 to 6
- tangent_values: bfloat16 [16384, 8, 128], P('ctx', 'head'), may hold values from -6 to 6
- doc_start: int32 [128], P('ctx'), may hold values from 0 to 127, as said below
- out_gain: float32 [4096], P('head'), may hold values from 0.1 to 1.9
Outputs:
- product_queries: float32 [16384, 32, 128], P('ctx', 'head')
- product_keys: float32 [16384, 8, 128], P('ctx', 'head')
- product_values: float32 [16384, 8, 128], P('ctx', 'head')
The draws below stay inside these ranges and needn't reach their ends.
Inputs may be any that keep to these rules, and one draw needn't show every extreme that they name: Documents are runs of whole mask blocks; doc_start[b] is the first block of b's document, so it never falls and doc_start[b] <= b. No document is longer than 16 blocks, and one is exactly 16 blocks long.
All inputs are finite; a program needn't handle non-finite values.
Results may differ from the reference program's by a relative error of at most 0.014.
Values may be sent and summed in bfloat16 or wider, within the bound.
A program may use at most 64 MiB of HBM per device.

```python
import jax
import jax.numpy as jnp
from jax import lax

QH = 32
KVH = 8
HD = 128
TOK_DEV = 256
BLOCK = 128
DOC_DEVS = 8
TOKENS = 16384
DOC_BLOCKS = 16


def paired_rows(key):
    base = jax.random.fold_in(key, 11)
    key_rows = jnp.clip(jax.random.normal(jax.random.fold_in(base, 1), (TOKENS, KVH, HD), jnp.float32), -5.0, 5.0)
    query_rows = jnp.clip(jax.random.normal(jax.random.fold_in(base, 2), (TOKENS, QH, HD), jnp.float32), -5.0, 5.0)
    return (query_rows, key_rows)


def draw_queries(key, part):
    return paired_rows(key)[0].astype(jnp.bfloat16)


def draw_keys(key, part):
    return paired_rows(key)[1].astype(jnp.bfloat16)


def draw_values(key, part):
    base = jax.random.fold_in(key, 23)
    raw = jnp.clip(jax.random.normal(jax.random.fold_in(base, 1), (TOKENS, KVH, HD), jnp.float32), -5.0, 5.0)
    columns = jnp.exp(jax.random.uniform(jax.random.fold_in(base, 2), (1, KVH, HD), jnp.float32, 0.0, 2.302585))
    ladder = jnp.arange(KVH, dtype=jnp.float32) / (KVH - 1)
    rise = 3.0 ** (0.5 * ladder)
    return (raw * columns * rise[None, :, None]).astype(jnp.bfloat16)


def draw_doc_start(key, part):
    blocks = TOKENS // BLOCK
    longest = DOC_BLOCKS
    per_device = TOK_DEV // BLOCK
    lengths = jax.random.randint(jax.random.fold_in(key, 31), (blocks,), 1, longest + 1)
    starts = jnp.cumsum(lengths) - lengths
    marks = jnp.zeros((blocks + 1,), jnp.int32).at[jnp.minimum(starts, blocks)].set(1)[:blocks]
    slots = (blocks - longest - 1) // per_device + 1
    pick = jax.random.randint(jax.random.fold_in(key, 37), (), 0, slots) * per_device + 1
    places = jnp.arange(blocks)
    inside = (places > pick) & (places < pick + longest)
    marks = jnp.where(inside, 0, marks)
    marks = jnp.where((places == pick) | (places == pick + longest), 1, marks)
    return lax.cummax(jnp.where(marks == 1, places, 0), axis=0).astype(jnp.int32)


def levels(stream_key, shape, split, low, largest):
    loudness, own = 1.0, jax.random.fold_in(stream_key, 6)
    for dim, parts in split:
        steps = jnp.exp(jax.random.uniform(jax.random.fold_in(own, dim), (parts,), jnp.float32, low / len(split), largest / len(split)))
        loudness = loudness * jnp.repeat(steps, shape[dim] // parts).reshape([-1 if axis == dim else 1 for axis in range(len(shape))])
    return loudness


def bell_draw(stream_key, extent, deviation, bound, split=(), kind=jnp.bfloat16):
    values = jax.random.normal(stream_key, extent, jnp.float32) * deviation
    if len(split) > 0:
        values = levels(stream_key, extent, split, -0.22, 0.18) * values
    return jnp.clip(values, min=-bound, max=bound).astype(kind)


def setup_inputs(seed: int = 0) -> dict:
    arg_keys = jax.random.split(jax.random.key(seed), 9)
    return {
        "queries": draw_queries(jax.random.fold_in(arg_keys[8], 71), 0),
        "keys": draw_keys(jax.random.fold_in(arg_keys[8], 71), 0),
        "values": draw_values(jax.random.fold_in(arg_keys[8], 71), 0),
        "tangent_queries": bell_draw(arg_keys[3], (TOKENS, QH, HD), 1.0, 6.0, ((0, 64), (1, 8))),
        "tangent_keys": bell_draw(arg_keys[4], (TOKENS, KVH, HD), 1.0, 6.0, ((0, 64), (1, 8))),
        "tangent_values": bell_draw(arg_keys[5], (TOKENS, KVH, HD), 1.0, 6.0, ((0, 64), (1, 8))),
        "doc_start": draw_doc_start(jax.random.fold_in(arg_keys[8], 71), 0),
        "out_gain": jnp.clip(1.0 + 0.18 * jax.random.normal(arg_keys[7], (QH * HD,), jnp.float32), 0.1, 1.9),
    }


EPSILON = 1e-06

def rounded(entries):
    return lax.optimization_barrier(entries.astype(jnp.bfloat16)).astype(jnp.float32)

def reference(queries, keys, values, tangent_queries, tangent_keys, tangent_values, doc_start, out_gain):
    group = QH // KVH
    scale = HD ** (-0.5)
    rows = TOK_DEV
    span = rows + DOC_DEVS * TOK_DEV
    count = TOKENS // rows
    features = QH * HD
    starts = jnp.repeat(doc_start * BLOCK, BLOCK)
    query_float = queries.astype(jnp.float32).reshape(TOKENS, KVH, group, HD)
    slope_query = tangent_queries.astype(jnp.float32).reshape(TOKENS, KVH, group, HD)
    key_float = keys.astype(jnp.float32)
    value_float = values.astype(jnp.float32)
    slope_key = tangent_keys.astype(jnp.float32)
    slope_value = tangent_values.astype(jnp.float32)
    gain_heads = out_gain.reshape(KVH, group, 1, HD)

    def first_key(number):
        return jnp.clip(number * rows + rows - span, 0, TOKENS - span).astype(jnp.int32)

    def query_block(array, number):
        return lax.dynamic_slice_in_dim(array, (number * rows).astype(jnp.int32), rows, 0).transpose(1, 2, 0, 3)

    def key_block(array, first):
        return lax.dynamic_slice_in_dim(array, first, span, 0)

    def allowed_at(number, first):
        query_pos = number * rows + jnp.arange(rows, dtype=jnp.int32)
        key_pos = first + jnp.arange(span, dtype=jnp.int32)
        own_start = lax.dynamic_slice_in_dim(starts, (number * rows).astype(jnp.int32), rows, 0)
        return (key_pos[None, :] >= own_start[:, None]) & (key_pos[None, :] <= query_pos[:, None])

    def forward_block(number):
        first = first_key(number)
        allowed = allowed_at(number, first)
        query_here = query_block(query_float, number)
        slope_here = query_block(slope_query, number)
        key_here = key_block(key_float, first)
        value_here = key_block(value_float, first)
        key_slope = key_block(slope_key, first)
        value_slope = key_block(slope_value, first)
        scores = scale * jnp.einsum('kgtd,ukd->kgtu', query_here, key_here)
        slopes = scale * (jnp.einsum('kgtd,ukd->kgtu', slope_here, key_here) + jnp.einsum('kgtd,ukd->kgtu', query_here, key_slope))
        most = lax.optimization_barrier(jnp.max(jnp.where(allowed, scores, -jnp.inf), axis=-1))
        weights = jnp.where(allowed, jnp.exp(scores - most[..., None]), 0.0)
        total = lax.optimization_barrier(jnp.sum(weights, axis=-1))
        weighted = lax.optimization_barrier(jnp.sum(weights * slopes, axis=-1))
        weights_b = rounded(weights)
        mixed_b = rounded(weights * slopes)
        plain = jnp.einsum('kgtu,ukd->kgtd', weights_b, value_here)
        moving = jnp.einsum('kgtu,ukd->kgtd', mixed_b, value_here) + jnp.einsum('kgtu,ukd->kgtd', weights_b, value_slope)
        output = plain / total[..., None]
        moved = moving / total[..., None] - (weighted / total)[..., None] * output
        return (output, moved, most + jnp.log(total))
    numbers = jnp.arange(count, dtype=jnp.int32)
    output, moved, log_norm = lax.map(forward_block, numbers)

    def spread_rows(stat):
        return stat[:, None, None, :, None]
    square = lax.optimization_barrier(jnp.sum(output * output, axis=(1, 2, 4))) / features + EPSILON
    cross = lax.optimization_barrier(jnp.sum(output * moved, axis=(1, 2, 4)))
    root = jnp.sqrt(square)
    tangent_y = gain_heads * (moved - output * spread_rows(cross / (features * square))) / spread_rows(root)
    grad_out = gain_heads * tangent_y
    back = lax.optimization_barrier(jnp.sum(output * grad_out, axis=(1, 2, 4)))
    cotangent = rounded((grad_out - output * spread_rows(back / (features * square))) / spread_rows(root))
    row_dot = lax.optimization_barrier(jnp.sum(cotangent * output, axis=-1))

    def backward_block(carry, inputs):
        key_grad, value_grad = carry
        number, norm_here, cot_here, dot_here = inputs
        first = first_key(number)
        allowed = allowed_at(number, first)
        query_here = query_block(query_float, number)
        key_here = key_block(key_float, first)
        value_here = key_block(value_float, first)
        scores = scale * jnp.einsum('kgtd,ukd->kgtu', query_here, key_here)
        probs = jnp.where(allowed, jnp.exp(scores - norm_here[..., None]), 0.0)
        prob_dot = jnp.einsum('kgtd,ukd->kgtu', cot_here, value_here)
        score_grad = rounded(probs * (prob_dot - dot_here[..., None]) * scale)
        query_part = jnp.einsum('kgtu,ukd->kgtd', score_grad, key_here)
        key_part = jnp.einsum('kgtu,kgtd->ukd', score_grad, query_here)
        value_part = jnp.einsum('kgtu,kgtd->ukd', rounded(probs), cot_here)
        key_grad = lax.dynamic_update_slice_in_dim(key_grad, lax.dynamic_slice_in_dim(key_grad, first, span, 0) + key_part, first, 0)
        value_grad = lax.dynamic_update_slice_in_dim(value_grad, lax.dynamic_slice_in_dim(value_grad, first, span, 0) + value_part, first, 0)
        return ((key_grad, value_grad), query_part)
    empty = jnp.zeros((TOKENS, KVH, HD), jnp.float32)
    (product_keys, product_values), query_parts = lax.scan(backward_block, (empty, empty), (numbers, log_norm, cotangent, row_dot))
    product_queries = query_parts.transpose(0, 3, 1, 2, 4).reshape(TOKENS, QH, HD)
    return (product_queries, product_keys, product_values)
```

```python
import functools

import jax
import jax.numpy as jnp
from jax import lax
from jax.experimental import pallas as pl
from jax.experimental.pallas import tpu as pltpu
from jax.sharding import PartitionSpec as P

MESH = pl.DeviceIdType.MESH
FEATURES = 4096
EPSILON = 1e-06
LOG2E = 1.4426950408889634
MASKED = -1e30
ROWS = 1024
TILE = 256
TOK = 256
HD = 128

F32 = jnp.float32
BF16 = jnp.bfloat16

PHASES = (
    ((0, 0, 256),),
    ((1, 0, 256), (2, 0, 256)),
    ((3, 128, 128), (4, 0, 256)),
    ((5, 0, 128), (6, 0, 128)),
    ((7, 0, 128), (8, 0, 128)),
    ((5, 128, 128), (6, 128, 128)),
    ((7, 128, 128), (8, 128, 128)),
)
LAST = len(PHASES) - 1
CHUNKS = 4


def joined(pieces):
    return pieces[0] if len(pieces) == 1 else jnp.concatenate(pieces, axis=0)


def dot_nt(a, b):
    return lax.dot_general(a, b, (((1,), (1,)), ((), ())), preferred_element_type=F32)


def dot_tn(a, b):
    return lax.dot_general(a, b, (((0,), (0,)), ((), ())), preferred_element_type=F32)


def dot(a, b):
    return lax.dot_general(a, b, (((1,), (0,)), ((), ())), preferred_element_type=F32)


def split(x):
    hi = x.astype(BF16)
    return hi, (x - hi.astype(F32)).astype(BF16)


def kernel(
    contexts, heads,
    q_in, k_in, v_in, tq_in, tk_in, tv_in, doc_in, gain_in,
    dq_out, dk_out, dv_out,
    doc_ref, gain_ref, blocks, tqq, kept, most, acc, norms, grads, gains, pick, stat_out, stat_in,
    scaled, slope, parts, back_out, back_in,
    load_sem, fwd_send, fwd_recv, stat_send, stat_recv, back_send, back_recv,
):
    c = lax.axis_index("ctx")
    h = lax.axis_index("head")
    core = lax.rem(c, 2)
    scale = HD ** (-0.5)

    def ctx(shift):
        return (lax.rem(c + contexts + shift, contexts), h)

    partner = (c + 1 - 2 * core, h)
    mates = [(c, lax.rem(h + i, heads)) for i in range(1, heads)]
    barrier = pltpu.get_barrier_semaphore()
    peers = [ctx(2), ctx(-2), ctx(4), ctx(-4), partner] + mates
    for peer in peers:
        pl.semaphore_signal(barrier, inc=1, device_id=peer, device_id_type=MESH)

    loads = []
    places = (
        (k_in, blocks.at[0, :, 0:128]), (tk_in, blocks.at[0, :, 128:256]),
        (v_in, blocks.at[0, :, 256:384]), (tv_in, blocks.at[0, :, 384:512]),
        (tq_in, tqq.at[:, 0:128]), (q_in, tqq.at[:, 128:256]), (doc_in, doc_ref), (gain_in, gain_ref),
    )
    for i, (src, dst) in enumerate(places):
        load = pltpu.make_async_copy(src, dst, load_sem.at[i])
        load.start()
        loads.append(load)

    def remote(src, dst, send, recv, peer):
        return pltpu.make_async_remote_copy(
            src_ref=src, dst_ref=dst, send_sem=send, recv_sem=recv, device_id=peer, device_id_type=MESH
        )

    count = iter(range(100))

    def fwd(src, dst, peer, chunks):
        copies = []
        for j in range(chunks):
            rows = pl.ds(j * (TOK // chunks), TOK // chunks)
            i = next(count)
            copies.append(remote(
                blocks.at[src, rows], blocks.at[dst, rows], fwd_send.at[i], fwd_recv.at[i], peer
            ))
        return copies

    cross = fwd(0, 5, ctx(2), CHUNKS)
    hop6 = fwd(5, 7, ctx(4), CHUNKS)
    side2 = fwd(5, 6, partner, CHUNKS)
    side6 = fwd(7, 8, partner, CHUNKS)
    (hop4,), (hop8,) = fwd(0, 1, ctx(4), 1), fwd(1, 3, ctx(4), 1)
    (side4,), (side8,) = fwd(1, 2, partner, 1), fwd(3 * core, 4, partner, 1)

    offsets = (0, 4, 3 + 2 * core, 8, 7 - 6 * core, 2, 1 + 2 * core, 6, 5 + 2 * core)

    for load in loads[:4]:
        load.wait()
    pl.semaphore_wait(barrier, len(peers))
    for copy in cross:
        copy.start()
    hop4.start()
    for load in loads[4:]:
        load.wait()

    gain = gain_ref[...]
    four = jnp.concatenate([gain[:, 128 * i : 128 * i + 128] for i in range(4)], axis=0)
    eight = jnp.concatenate([four, four], axis=0)
    eight = eight * eight
    for i in range(512 // 8):
        gains[pl.ds(i * 8, 8), :] = eight
    row_token = lax.broadcasted_iota(jnp.int32, (512, 128), 0) // 4
    lane = lax.broadcasted_iota(jnp.int32, (512, 128), 1)
    pick[...] = jnp.where(row_token == lane, 1.0, 0.0).astype(BF16)
    parts[3, 0:128, :] = jnp.zeros((128, 256), F32)

    def forward(phase, low=0, high=ROWS // TILE):
        pieces_of = PHASES[phase]

        def step(i, carry):
            rows = pl.ds(pl.multiple_of(i * TILE, TILE), TILE)
            first = doc_ref[i // 2]
            both = tqq[rows, :]
            keys = joined([blocks[s, r : r + n, 0:256] for s, r, n in pieces_of])
            vals = joined([blocks[s, r : r + n, 256:512] for s, r, n in pieces_of])
            scores = dot_nt(both[:, 128:256], keys[:, 0:128]) * (scale * LOG2E)
            slopes = dot_nt(both, keys)
            pieces = []
            for s, r, n in pieces_of:
                for block in range(r // 128, (r + n) // 128):
                    j = len(pieces)
                    kb = 2 * (c - offsets[s]) + block
                    piece = scores[:, 128 * j : 128 * j + 128]
                    piece = piece + jnp.where(kb >= first, 0.0, MASKED).astype(F32)
                    if phase == 0:
                        token = i * (TILE // 4) + lax.broadcasted_iota(jnp.int32, (TILE, 128), 0) // 4
                        key = 128 * block + lax.broadcasted_iota(jnp.int32, (TILE, 128), 1)
                        piece = jnp.where(key <= token, piece, MASKED)
                    pieces.append(piece)
            top = pieces[0]
            for piece in pieces[1:]:
                top = jnp.maximum(top, piece)
            new = jnp.max(top, axis=1, keepdims=True)
            if phase > 0:
                old = most[phase - 1, rows, :][:, 0:1]
                new = jnp.maximum(old, new)
                decay = jnp.exp2(old - new)
            most[phase, rows, :] = jnp.broadcast_to(new, (TILE, 128))
            total = jnp.zeros((TILE, 128), F32)
            weighted = jnp.zeros((TILE, 128), F32)
            plain, mixed = [], []
            for j, piece in enumerate(pieces):
                weight = jnp.exp2(piece - new)
                mix = weight * slopes[:, 128 * j : 128 * j + 128]
                total = total + weight
                weighted = weighted + mix
                plain.append(weight.astype(BF16))
                mixed.append(mix.astype(BF16))
            plain = jnp.concatenate(plain, axis=1)
            mixed = jnp.concatenate(mixed, axis=1)
            at = 0
            for s, r, n in pieces_of:
                kept[rows, s * TOK + r : s * TOK + r + n] = plain[:, at : at + n]
                at += n
            product = dot(plain, vals)
            moving = product[:, 128:256] + scale * dot(mixed, vals[:, 0:128])
            stable = product[:, 0:128]
            if phase > 0:
                stable = stable + acc[rows, 0:128] * decay
                moving = moving + acc[rows, 128:256] * decay
                total = total + norms[rows, 0:128] * decay
                weighted = weighted + norms[rows, 128:256] * decay
            acc[rows, 0:128] = stable
            acc[rows, 128:256] = moving
            norms[rows, 0:128] = total
            norms[rows, 128:256] = weighted
            return carry

        lax.fori_loop(low, high, step, 0)

    def stat_copy(half, i):
        return remote(
            stat_out.at[half], stat_in.at[half, h],
            stat_send.at[half * heads + i], stat_recv.at[half * heads + h], mates[i - 1],
        )

    def stat_arrival(half, source):
        return remote(
            stat_out.at[half], stat_in.at[half, source],
            stat_send.at[half * heads], stat_recv.at[half * heads + source], mates[0],
        )

    def finish(half):
        rows = pl.ds(half * 512, 512)
        inverse = 1.0 / jnp.sum(norms[rows, 0:128], axis=1, keepdims=True)
        center = jnp.sum(norms[rows, 128:256], axis=1, keepdims=True) * scale
        output = acc[rows, 0:128] * inverse
        moved = acc[rows, 128:256] * inverse - (center * inverse) * output
        acc[rows, 0:128] = output
        acc[rows, 128:256] = moved
        norms[rows, 0:128] = jnp.broadcast_to(inverse, (512, 128))
        squared = gains[...]
        square = output * output
        cross_term = output * moved
        terms = [split(x) for x in (square, cross_term, squared * cross_term, squared * square)]
        right = jnp.concatenate([t[0] for t in terms] + [t[1] for t in terms], axis=1)
        line = lax.broadcasted_iota(jnp.int32, (8, 1024), 0)
        place = lax.broadcasted_iota(jnp.int32, (8, 1024), 1) // 128
        left = jnp.where(lax.rem(place, 4) == line, 1.0, 0.0).astype(BF16)
        per_row = dot_nt(left, right)
        hi, lo = split(per_row)
        stat_out[half] = dot(hi, pick[...]) + dot(lo, pick[...])
        for i in range(1, heads):
            stat_copy(half, i).start()

    def cotangent(half):
        rows = pl.ds(half * 512, 512)
        sums = stat_out[half]
        for i in range(1, heads):
            source = lax.rem(h + i, heads)
            stat_arrival(half, source).wait_recv()
            sums = sums + stat_in[half, source]
        inverse_square = 1.0 / (sums[0:1] / FEATURES + EPSILON)
        along = inverse_square * sums[1:2] / FEATURES
        back = inverse_square * inverse_square * (sums[2:3] - along * sums[3:4]) / FEATURES
        sides = []
        for value in (inverse_square, along, back):
            wide = jnp.broadcast_to(value, (128, 128))
            hi, lo = split(wide)
            sides.append(jnp.concatenate([hi, lo], axis=1))
        both = jnp.concatenate([pick[...], pick[...]], axis=1)
        spread = dot_nt(both, jnp.concatenate(sides, axis=0))
        output = acc[rows, 0:128]
        moved = acc[rows, 128:256]
        grads[rows, :] = (
            spread[:, 0:128] * (gains[...] * (moved - spread[:, 128:256] * output))
            - spread[:, 256:384] * output
        )

    forward(0)
    hop4.wait_recv()
    hop8.start()
    side4.start()
    side4.wait_recv()
    forward(1)
    hop8.wait_recv()
    side8.start()
    side8.wait_recv()
    forward(2)
    for part in range(2):
        span = range(part * CHUNKS // 2, (part + 1) * CHUNKS // 2)
        for j in span:
            cross[j].wait_recv()
            hop6[j].start()
            side2[j].start()
        for j in span:
            side2[j].wait_recv()
        forward(3 + 2 * part)
        for j in span:
            hop6[j].wait_recv()
            side6[j].start()
        for j in span:
            side6[j].wait_recv()
        if part == 0:
            forward(4)
    forward(LAST, 0, 2)
    finish(0)
    forward(LAST, 2, 4)
    finish(1)

    def backward_rows(phase, first, low=0, high=ROWS // TILE):
        pieces_of = PHASES[phase]
        width = sum(n for s, r, n in pieces_of)
        spot = phase // 2 % 2

        def step(i, carry):
            rows = pl.ds(pl.multiple_of(i * TILE, TILE), TILE)
            keys = joined([blocks[s, r : r + n, 0:128] for s, r, n in pieces_of])
            vals = joined([blocks[s, r : r + n, 256:384] for s, r, n in pieces_of])
            factor = norms[rows, 0:1]
            if phase < LAST:
                factor = factor * jnp.exp2(most[phase, rows, :][:, 0:1] - most[LAST, rows, :][:, 0:1])
            part = (factor * grads[rows, :]).astype(BF16)
            scaled[spot, rows, :] = part
            row_dot = jnp.sum(part.astype(F32) * acc[rows, 0:128], axis=1, keepdims=True)
            weight = jnp.concatenate([kept[rows, s * TOK + r : s * TOK + r + n] for s, r, n in pieces_of], axis=1)
            grad = (weight.astype(F32) * (dot_nt(part, vals) - row_dot)).astype(BF16)
            slope[spot, rows, 0:width] = grad
            product = dot(grad, keys) * scale
            if first:
                dq_out[rows, :] = product
            else:
                dq_out[rows, :] = dq_out[rows, :] + product
            return carry

        lax.fori_loop(low, high, step, 0)

    def backward_keys(phase):
        spot = phase // 2 % 2
        at = 0
        for s, r, n in PHASES[phase]:
            parts[s, r : r + n, 0:128] = dot_tn(slope[spot, :, at : at + n], tqq[:, 128:256]) * scale
            parts[s, r : r + n, 128:256] = dot_tn(kept[:, s * TOK + r : s * TOK + r + n], scaled[spot])
            at += n

    def backward(phase):
        backward_rows(phase, False)
        backward_keys(phase)

    tags = iter(range(100))

    def back(i, peer, chunks=1):
        copies = []
        for j in range(chunks):
            rows = pl.ds(j * (TOK // chunks), TOK // chunks)
            tag = next(tags)
            copy = remote(
                back_out.at[i, rows], back_in.at[i, rows], back_send.at[tag], back_recv.at[tag], peer
            )
            copies.append((copy, i, slice(j * (TOK // chunks), (j + 1) * (TOK // chunks))))
        return copies

    side_back = [back(0, partner), back(1, partner), back(2, partner, 2), back(3, partner, 2)]
    home6, home8, home4 = back(4, ctx(-4), 2), back(5, ctx(-4)), back(6, ctx(-4))
    home2 = back(7, ctx(-2), 2)

    def send(item, value):
        copy, i, rows = item
        back_out[i, rows, :] = value.astype(BF16)
        copy.start()

    def got(item):
        copy, i, rows = item
        copy.wait_recv()
        return back_in[i, rows, :].astype(F32)

    on_one = jnp.where(core == 1, 1.0, 0.0).astype(F32)
    half = (slice(0, 128), slice(128, 256))
    cotangent(0)
    backward_rows(4, True, 0, 2)
    backward_rows(6, False, 0, 2)
    cotangent(1)
    backward_rows(4, True, 2, 4)
    backward_keys(4)
    send(side_back[3][0], parts[8, half[0], :])
    backward_rows(6, False, 2, 4)
    backward_keys(6)
    send(side_back[3][1], parts[8, half[1], :])
    send(home6[0], parts[7, half[0], :] + got(side_back[3][0]))
    backward(3)
    send(side_back[2][0], parts[6, half[0], :])
    send(home6[1], parts[7, half[1], :] + got(side_back[3][1]))
    backward(5)
    send(side_back[2][1], parts[6, half[1], :])
    for j in range(2):
        send(home2[j], parts[5, half[j], :] + got(side_back[2][j]) + got(home6[j]))
    backward(2)
    send(side_back[1][0], parts[4])
    shared = got(side_back[1][0])
    send(home8[0], parts[3] + on_one * shared)
    backward(1)
    send(side_back[0][0], parts[2])
    send(home4[0], parts[1] + got(side_back[0][0]) + got(home8[0]))
    backward(0)
    own = parts[0] + (1.0 - on_one) * back_in[1].astype(F32) + got(home4[0])
    for j in range(2):
        total = own[half[j], :] + got(home2[j])
        dk_out[half[j], :] = total[:, 0:128]
        dv_out[half[j], :] = total[:, 128:256]

    for copy in cross + [hop4, hop8] + hop6 + [side4, side8] + side2 + side6:
        copy.wait_send()
    for part in range(2):
        for i in range(1, heads):
            stat_copy(part, i).wait_send()
    for group in side_back + [home6, home8, home4, home2]:
        for copy, _, _ in group:
            copy.wait_send()


def hand_on(*refs):
    ins, outs, held, sems = refs[0:3], refs[3:6], refs[6:9], refs[9]
    copies = []
    for i in range(3):
        copies.append((
            pltpu.make_async_copy(ins[i], held[i], sems.at[0, i]),
            pltpu.make_async_copy(held[i], outs[i], sems.at[1, i]),
        ))
    for into, _ in copies:
        into.start()
    for into, out in copies:
        into.wait()
        out.start()
    for _, out in copies:
        out.wait()


def solution(mesh):
    contexts, heads = mesh.shape["ctx"], mesh.shape["head"]

    def body(queries, keys, values, tangent_queries, tangent_keys, tangent_values, doc_start, out_gain):
        any_space = pl.BlockSpec(memory_space=pl.ANY)
        vmem = pl.BlockSpec(memory_space=pltpu.VMEM)
        sems = pltpu.SemaphoreType.DMA
        dq, dk, dv = pl.pallas_call(
            functools.partial(kernel, contexts, heads),
            name="gauss_newton",
            out_shape=(
                jax.ShapeDtypeStruct((ROWS, HD), F32),
                jax.ShapeDtypeStruct((TOK, HD), F32),
                jax.ShapeDtypeStruct((TOK, HD), F32),
            ),
            in_specs=[any_space] * 8,
            out_specs=(vmem, vmem, vmem),
            scratch_shapes=[
                pltpu.SMEM((2,), jnp.int32),
                pltpu.VMEM((1, 512), F32),
                pltpu.VMEM((9, TOK, 512), BF16),
                pltpu.VMEM((ROWS, 256), BF16),
                pltpu.VMEM((ROWS, 9 * TOK), BF16),
                pltpu.VMEM((len(PHASES), ROWS, 128), F32),
                pltpu.VMEM((ROWS, 256), F32),
                pltpu.VMEM((ROWS, 256), F32),
                pltpu.VMEM((ROWS, 128), F32),
                pltpu.VMEM((512, 128), F32),
                pltpu.VMEM((512, 128), BF16),
                pltpu.VMEM((2, 8, 128), F32),
                pltpu.VMEM((2, heads, 8, 128), F32),
                pltpu.VMEM((2, ROWS, 128), BF16),
                pltpu.VMEM((2, ROWS, 512), BF16),
                pltpu.VMEM((9, TOK, 256), F32),
                pltpu.VMEM((8, TOK, 256), BF16),
                pltpu.VMEM((8, TOK, 256), BF16),
                sems((8,)), sems((4 * CHUNKS + 4,)), sems((4 * CHUNKS + 4,)),
                sems((2 * heads,)), sems((2 * heads,)), sems((12,)), sems((12,)),
            ],
            compiler_params=pltpu.CompilerParams(
                collective_id=0, has_side_effects=True, vmem_limit_bytes=60 * 1024 * 1024
            ),
        )(
            queries.reshape(ROWS, HD), keys.reshape(TOK, HD), values.reshape(TOK, HD),
            tangent_queries.reshape(ROWS, HD), tangent_keys.reshape(TOK, HD),
            tangent_values.reshape(TOK, HD), doc_start, out_gain.reshape(1, 512),
        )
        dq, dk, dv = pl.pallas_call(
            hand_on,
            name="hand_on",
            out_shape=tuple(jax.ShapeDtypeStruct(x.shape, F32) for x in (dq, dk, dv)),
            in_specs=[any_space] * 3,
            out_specs=(any_space,) * 3,
            scratch_shapes=[pltpu.VMEM(x.shape, F32) for x in (dq, dk, dv)] + [sems((2, 3))],
        )(dq, dk, dv)
        return dq.reshape(TOK, 4, HD), dk.reshape(TOK, 1, HD), dv.reshape(TOK, 1, HD)

    wide = P("ctx", "head", None)
    return jax.shard_map(
        body,
        mesh=mesh,
        in_specs=(wide, wide, wide, wide, wide, wide, P("ctx"), P("head")),
        out_specs=(wide, wide, wide),
        check_vma=False,
    )
```

```python
import functools

import jax
import jax.numpy as jnp
from jax import lax
from jax.experimental import pallas as pl
from jax.experimental.pallas import tpu as pltpu
from jax.sharding import PartitionSpec as P

MESH = pl.DeviceIdType.MESH
FEATURES = 4096
EPSILON = 1e-06
LOG2E = 1.4426950408889634
MASKED = -1e30
ROWS = 1024
TILE = 512
TOK = 256
HD = 128

F32 = jnp.float32
BF16 = jnp.bfloat16

PHASES = (
    ((0, 0, 256),),
    ((1, 0, 256), (2, 0, 256)),
    ((3, 128, 128), (4, 0, 256)),
    ((5, 0, 256), (6, 0, 256)),
    ((7, 0, 256), (8, 0, 256)),
)
LAST = len(PHASES) - 1
CHUNKS = 8
BACK = 4


def joined(pieces):
    return pieces[0] if len(pieces) == 1 else jnp.concatenate(pieces, axis=0)


def dot_nt(a, b):
    return lax.dot_general(a, b, (((1,), (1,)), ((), ())), preferred_element_type=F32)


def dot_tn(a, b):
    return lax.dot_general(a, b, (((0,), (0,)), ((), ())), preferred_element_type=F32)


def dot(a, b):
    return lax.dot_general(a, b, (((1,), (0,)), ((), ())), preferred_element_type=F32)


def split(x):
    hi = x.astype(BF16)
    return hi, (x - hi.astype(F32)).astype(BF16)


def kernel(
    contexts, heads,
    q_in, k_in, v_in, tq_in, tk_in, tv_in, doc_in, gain_in,
    dq_out, dk_out, dv_out,
    doc_ref, gain_ref, blocks, tqq, kept, most, acc, norms, grads, gains, pick, stat_out, stat_in,
    scaled, slope, parts, back_out, back_in,
    dq_held, load_sem, fwd_send, fwd_recv, stat_send, stat_recv, back_send, back_recv,
):
    c = lax.axis_index("ctx")
    h = lax.axis_index("head")
    core = lax.rem(c, 2)
    scale = HD ** (-0.5)

    def ctx(shift):
        return (lax.rem(c + contexts + shift, contexts), h)

    partner = (c + 1 - 2 * core, h)
    mates = [(c, lax.rem(h + i, heads)) for i in range(1, heads)]
    barrier = pltpu.get_barrier_semaphore()
    peers = [ctx(2), ctx(-2), ctx(4), ctx(-4), partner] + mates
    for peer in peers:
        pl.semaphore_signal(barrier, inc=1, device_id=peer, device_id_type=MESH)

    loads = []
    places = (
        (k_in, blocks.at[0, :, 0:128]), (tk_in, blocks.at[0, :, 128:256]),
        (v_in, blocks.at[0, :, 256:384]), (tv_in, blocks.at[0, :, 384:512]),
        (tq_in, tqq.at[:, 0:128]), (q_in, tqq.at[:, 128:256]), (doc_in, doc_ref), (gain_in, gain_ref),
    )
    for i, (src, dst) in enumerate(places):
        load = pltpu.make_async_copy(src, dst, load_sem.at[i])
        load.start()
        loads.append(load)

    def remote(src, dst, send, recv, peer):
        return pltpu.make_async_remote_copy(
            src_ref=src, dst_ref=dst, send_sem=send, recv_sem=recv, device_id=peer, device_id_type=MESH
        )

    count = iter(range(100))

    def fwd(src, dst, peer, chunks):
        copies = []
        for j in range(chunks):
            rows = pl.ds(j * (TOK // chunks), TOK // chunks)
            i = next(count)
            copies.append(remote(
                blocks.at[src, rows], blocks.at[dst, rows], fwd_send.at[i], fwd_recv.at[i], peer
            ))
        return copies

    cross = fwd(0, 5, ctx(2), CHUNKS)
    hop6 = fwd(5, 7, ctx(4), CHUNKS)
    side2 = fwd(5, 6, partner, CHUNKS)
    side6 = fwd(7, 8, partner, CHUNKS)
    (hop4,), (hop8,) = fwd(0, 1, ctx(4), 1), fwd(1, 3, ctx(4), 1)
    (side4,), (side8,) = fwd(1, 2, partner, 1), fwd(3 * core, 4, partner, 1)

    offsets = (0, 4, 3 + 2 * core, 8, 7 - 6 * core, 2, 1 + 2 * core, 6, 5 + 2 * core)

    for load in loads[:4]:
        load.wait()
    pl.semaphore_wait(barrier, len(peers))
    for copy in cross:
        copy.start()
    hop4.start()
    for load in loads[4:]:
        load.wait()

    gain = gain_ref[...]
    four = jnp.concatenate([gain[:, 128 * i : 128 * i + 128] for i in range(4)], axis=0)
    eight = jnp.concatenate([four, four], axis=0)
    eight = eight * eight
    for i in range(512 // 8):
        gains[pl.ds(i * 8, 8), :] = eight
    row_token = lax.broadcasted_iota(jnp.int32, (512, 128), 0) // 4
    lane = lax.broadcasted_iota(jnp.int32, (512, 128), 1)
    pick[...] = jnp.where(row_token == lane, 1.0, 0.0).astype(BF16)
    parts[3, 0:128, :] = jnp.zeros((128, 256), F32)

    def forward(phase, low=0, high=ROWS // TILE):
        pieces_of = PHASES[phase]

        def step(i, carry):
            rows = pl.ds(pl.multiple_of(i * TILE, TILE), TILE)
            first = doc_ref[i * TILE // 512]
            both = tqq[rows, :]
            keys = joined([blocks[s, r : r + n, 0:256] for s, r, n in pieces_of])
            vals = joined([blocks[s, r : r + n, 256:512] for s, r, n in pieces_of])
            scores = dot_nt(both[:, 128:256], keys[:, 0:128]) * (scale * LOG2E)
            slopes = dot_nt(both, keys)
            pieces = []
            for s, r, n in pieces_of:
                for block in range(r // 128, (r + n) // 128):
                    j = len(pieces)
                    kb = 2 * (c - offsets[s]) + block
                    piece = scores[:, 128 * j : 128 * j + 128]
                    piece = piece + jnp.where(kb >= first, 0.0, MASKED).astype(F32)
                    if phase == 0:
                        token = i * (TILE // 4) + lax.broadcasted_iota(jnp.int32, (TILE, 128), 0) // 4
                        key = 128 * block + lax.broadcasted_iota(jnp.int32, (TILE, 128), 1)
                        piece = jnp.where(key <= token, piece, MASKED)
                    pieces.append(piece)
            top = pieces[0]
            for piece in pieces[1:]:
                top = jnp.maximum(top, piece)
            new = jnp.max(top, axis=1, keepdims=True)
            if phase > 0:
                old = most[phase - 1, rows, :][:, 0:1]
                new = jnp.maximum(old, new)
                decay = jnp.exp2(old - new)
            most[phase, rows, :] = jnp.broadcast_to(new, (TILE, 128))
            total = jnp.zeros((TILE, 128), F32)
            weighted = jnp.zeros((TILE, 128), F32)
            plain, mixed = [], []
            for j, piece in enumerate(pieces):
                weight = jnp.exp2(piece - new)
                mix = weight * slopes[:, 128 * j : 128 * j + 128]
                total = total + weight
                weighted = weighted + mix
                plain.append(weight.astype(BF16))
                mixed.append(mix.astype(BF16))
            plain = jnp.concatenate(plain, axis=1)
            mixed = jnp.concatenate(mixed, axis=1)
            at = 0
            for s, r, n in pieces_of:
                kept[rows, s * TOK + r : s * TOK + r + n] = plain[:, at : at + n]
                at += n
            product = dot(plain, vals)
            moving = product[:, 128:256] + scale * dot(mixed, vals[:, 0:128])
            stable = product[:, 0:128]
            if phase > 0:
                stable = stable + acc[rows, 0:128] * decay
                moving = moving + acc[rows, 128:256] * decay
                total = total + norms[rows, 0:128] * decay
                weighted = weighted + norms[rows, 128:256] * decay
            acc[rows, 0:128] = stable
            acc[rows, 128:256] = moving
            norms[rows, 0:128] = total
            norms[rows, 128:256] = weighted
            return carry

        lax.fori_loop(low, high, step, 0)

    def stat_copy(half, i):
        return remote(
            stat_out.at[half], stat_in.at[half, h],
            stat_send.at[half * heads + i], stat_recv.at[half * heads + h], mates[i - 1],
        )

    def stat_arrival(half, source):
        return remote(
            stat_out.at[half], stat_in.at[half, source],
            stat_send.at[half * heads], stat_recv.at[half * heads + source], mates[0],
        )

    def finish(half):
        rows = pl.ds(half * 512, 512)
        inverse = 1.0 / jnp.sum(norms[rows, 0:128], axis=1, keepdims=True)
        center = jnp.sum(norms[rows, 128:256], axis=1, keepdims=True) * scale
        output = acc[rows, 0:128] * inverse
        moved = acc[rows, 128:256] * inverse - (center * inverse) * output
        acc[rows, 0:128] = output
        acc[rows, 128:256] = moved
        norms[rows, 0:128] = jnp.broadcast_to(inverse, (512, 128))
        squared = gains[...]
        square = output * output
        cross_term = output * moved
        terms = [split(x) for x in (square, cross_term, squared * cross_term, squared * square)]
        right = jnp.concatenate([t[0] for t in terms] + [t[1] for t in terms], axis=1)
        line = lax.broadcasted_iota(jnp.int32, (8, 1024), 0)
        place = lax.broadcasted_iota(jnp.int32, (8, 1024), 1) // 128
        left = jnp.where(lax.rem(place, 4) == line, 1.0, 0.0).astype(BF16)
        per_row = dot_nt(left, right)
        hi, lo = split(per_row)
        stat_out[half] = dot(hi, pick[...]) + dot(lo, pick[...])
        for i in range(1, heads):
            stat_copy(half, i).start()

    def cotangent(half):
        rows = pl.ds(half * 512, 512)
        sums = stat_out[half]
        for i in range(1, heads):
            source = lax.rem(h + i, heads)
            stat_arrival(half, source).wait_recv()
            sums = sums + stat_in[half, source]
        inverse_square = 1.0 / (sums[0:1] / FEATURES + EPSILON)
        along = inverse_square * sums[1:2] / FEATURES
        back = inverse_square * inverse_square * (sums[2:3] - along * sums[3:4]) / FEATURES
        sides = []
        for value in (inverse_square, along, back):
            wide = jnp.broadcast_to(value, (128, 128))
            hi, lo = split(wide)
            sides.append(jnp.concatenate([hi, lo], axis=1))
        both = jnp.concatenate([pick[...], pick[...]], axis=1)
        spread = dot_nt(both, jnp.concatenate(sides, axis=0))
        output = acc[rows, 0:128]
        moved = acc[rows, 128:256]
        grads[rows, :] = (
            spread[:, 0:128] * (gains[...] * (moved - spread[:, 128:256] * output))
            - spread[:, 256:384] * output
        )

    forward(0)
    hop4.wait_recv()
    hop8.start()
    side4.start()
    side4.wait_recv()
    forward(1)
    hop8.wait_recv()
    side8.start()
    for part in range(2):
        for j in range(part * CHUNKS // 2, (part + 1) * CHUNKS // 2):
            cross[j].wait_recv()
            hop6[j].start()
            side2[j].start()
        if part == 0:
            side8.wait_recv()
            forward(2)
    for j in range(CHUNKS // 2):
        hop6[j].wait_recv()
        side6[j].start()
    for j in range(CHUNKS):
        side2[j].wait_recv()
    forward(3)
    for j in range(CHUNKS // 2, CHUNKS):
        hop6[j].wait_recv()
        side6[j].start()
    for j in range(CHUNKS):
        side6[j].wait_recv()
    middle = 512 // TILE
    forward(LAST, 0, middle)
    finish(0)
    forward(LAST, middle, 2 * middle)
    finish(1)

    def backward_rows(phase, first, low=0, high=ROWS // TILE):
        pieces_of = PHASES[phase]
        width = sum(n for s, r, n in pieces_of)

        def step(i, carry):
            rows = pl.ds(pl.multiple_of(i * TILE, TILE), TILE)
            keys = joined([blocks[s, r : r + n, 0:128] for s, r, n in pieces_of])
            vals = joined([blocks[s, r : r + n, 256:384] for s, r, n in pieces_of])
            factor = norms[rows, 0:1]
            if phase < LAST:
                factor = factor * jnp.exp2(most[phase, rows, :][:, 0:1] - most[LAST, rows, :][:, 0:1])
            part = (factor * grads[rows, :]).astype(BF16)
            scaled[rows, :] = part
            row_dot = jnp.sum(part.astype(F32) * acc[rows, 0:128], axis=1, keepdims=True)
            weight = jnp.concatenate([kept[rows, s * TOK + r : s * TOK + r + n] for s, r, n in pieces_of], axis=1)
            grad = (weight.astype(F32) * (dot_nt(part, vals) - row_dot)).astype(BF16)
            slope[rows, 0:width] = grad
            product = dot(grad, keys) * scale
            if first:
                dq_held[rows, :] = product
            else:
                dq_held[rows, :] = dq_held[rows, :] + product
            return carry

        lax.fori_loop(low, high, step, 0)

    def backward_keys(phase, which):
        at = sum(n for _, _, n in PHASES[phase][:which])
        s, r, n = PHASES[phase][which]
        parts[s, r : r + n, 0:128] = dot_tn(slope[:, at : at + n], tqq[:, 128:256]) * scale
        parts[s, r : r + n, 128:256] = dot_tn(kept[:, s * TOK + r : s * TOK + r + n], scaled[...])

    tags = iter(range(100))

    def back(i, peer, chunks=1):
        copies = []
        for j in range(chunks):
            rows = pl.ds(j * (TOK // chunks), TOK // chunks)
            tag = next(tags)
            copy = remote(
                back_out.at[i, rows], back_in.at[i, rows], back_send.at[tag], back_recv.at[tag], peer
            )
            copies.append((copy, i, slice(j * (TOK // chunks), (j + 1) * (TOK // chunks))))
        return copies

    side_back = [back(0, partner), back(1, partner), back(2, partner, 2), back(3, partner, 2)]
    home6, home8, home4 = back(4, ctx(-4), BACK), back(5, ctx(-4)), back(6, ctx(-4))
    home2 = back(7, ctx(-2), BACK)

    def send(item, value):
        copy, i, rows = item
        back_out[i, rows, :] = value.astype(BF16)
        copy.start()

    def send_all(items, value):
        for item in items:
            send(item, value[item[2], :])

    def got_all(items):
        return joined([got(item) for item in items])

    def got(item):
        copy, i, rows = item
        copy.wait_recv()
        return back_in[i, rows, :].astype(F32)

    on_one = jnp.where(core == 1, 1.0, 0.0).astype(F32)
    quarter = [item[2] for item in home2]
    cotangent(0)
    backward_rows(4, True, 0, middle)
    cotangent(1)
    backward_rows(4, True, middle, 2 * middle)
    backward_keys(4, 1)
    send_all(side_back[3], parts[8])
    backward_keys(4, 0)
    for j in range(2):
        shared = got(side_back[3][j])
        for k in range(j * BACK // 2, (j + 1) * BACK // 2):
            at = quarter[k].start - j * 128
            send(home6[k], parts[7, quarter[k], :] + shared[at : at + TOK // BACK, :])
    backward_rows(3, False)
    backward_keys(3, 1)
    send_all(side_back[2], parts[6])
    backward_keys(3, 0)
    for j in range(2):
        shared = got(side_back[2][j])
        for k in range(j * BACK // 2, (j + 1) * BACK // 2):
            at = quarter[k].start - j * 128
            value = parts[5, quarter[k], :] + shared[at : at + TOK // BACK, :]
            send(home2[k], value + got(home6[k]))
    backward_rows(2, False)
    backward_keys(2, 1)
    send_all(side_back[1], parts[4])
    backward_keys(2, 0)
    send_all(home8, parts[3] + on_one * got_all(side_back[1]))
    backward_rows(1, False)
    backward_keys(1, 1)
    send_all(side_back[0], parts[2])
    backward_keys(1, 0)
    send_all(home4, parts[1] + got_all(side_back[0]) + got_all(home8))
    backward_rows(0, False)
    leave = pltpu.make_async_copy(dq_held, dq_out, load_sem.at[0])
    leave.start()
    backward_keys(0, 0)
    own = parts[0] + (1.0 - on_one) * back_in[1].astype(F32) + got_all(home4)
    parts[0] = own
    for k in range(BACK):
        total = parts[0, quarter[k], :] + got(home2[k])
        dk_out[quarter[k], :] = total[:, 0:128]
        dv_out[quarter[k], :] = total[:, 128:256]

    for copy in cross + [hop4, hop8] + hop6 + [side4, side8] + side2 + side6:
        copy.wait_send()
    for part in range(2):
        for i in range(1, heads):
            stat_copy(part, i).wait_send()
    leave.wait()
    for group in side_back + [home6, home8, home4, home2]:
        for copy, _, _ in group:
            copy.wait_send()


def hand_on(*refs):
    ins, outs, held, sems = refs[0:3], refs[3:6], refs[6:9], refs[9]
    copies = []
    for i in range(3):
        step = ROWS // 4 if i == 0 else TOK
        for j in range(ins[i].shape[0] // step):
            rows = pl.ds(j * step, step)
            at = len(copies)
            copies.append((
                pltpu.make_async_copy(ins[i].at[rows], held[i].at[rows], sems.at[0, at]),
                pltpu.make_async_copy(held[i].at[rows], outs[i].at[rows], sems.at[1, at]),
            ))
    for into, _ in copies:
        into.start()
    for into, out in copies:
        into.wait()
        out.start()
    for _, out in copies:
        out.wait()


def solution(mesh):
    contexts, heads = mesh.shape["ctx"], mesh.shape["head"]

    def body(queries, keys, values, tangent_queries, tangent_keys, tangent_values, doc_start, out_gain):
        any_space = pl.BlockSpec(memory_space=pl.ANY)
        vmem = pl.BlockSpec(memory_space=pltpu.VMEM)
        sems = pltpu.SemaphoreType.DMA
        dq, dk, dv = pl.pallas_call(
            functools.partial(kernel, contexts, heads),
            name="gauss_newton",
            out_shape=(
                jax.ShapeDtypeStruct((ROWS, HD), F32),
                jax.ShapeDtypeStruct((TOK, HD), F32),
                jax.ShapeDtypeStruct((TOK, HD), F32),
            ),
            in_specs=[any_space] * 8,
            out_specs=(any_space, vmem, vmem),
            scratch_shapes=[
                pltpu.SMEM((2,), jnp.int32),
                pltpu.VMEM((1, 512), F32),
                pltpu.VMEM((9, TOK, 512), BF16),
                pltpu.VMEM((ROWS, 256), BF16),
                pltpu.VMEM((ROWS, 9 * TOK), BF16),
                pltpu.VMEM((len(PHASES), ROWS, 128), F32),
                pltpu.VMEM((ROWS, 256), F32),
                pltpu.VMEM((ROWS, 256), F32),
                pltpu.VMEM((ROWS, 128), F32),
                pltpu.VMEM((512, 128), F32),
                pltpu.VMEM((512, 128), BF16),
                pltpu.VMEM((2, 8, 128), F32),
                pltpu.VMEM((2, heads, 8, 128), F32),
                pltpu.VMEM((ROWS, 128), BF16),
                pltpu.VMEM((ROWS, 512), BF16),
                pltpu.VMEM((9, TOK, 256), F32),
                pltpu.VMEM((8, TOK, 256), BF16),
                pltpu.VMEM((8, TOK, 256), BF16),
                pltpu.VMEM((ROWS, HD), F32),
                sems((8,)), sems((4 * CHUNKS + 4,)), sems((4 * CHUNKS + 4,)),
                sems((2 * heads,)), sems((2 * heads,)), sems((2 * BACK + 8,)), sems((2 * BACK + 8,)),
            ],
            compiler_params=pltpu.CompilerParams(
                collective_id=0, has_side_effects=True, vmem_limit_bytes=60 * 1024 * 1024
            ),
        )(
            queries.reshape(ROWS, HD), keys.reshape(TOK, HD), values.reshape(TOK, HD),
            tangent_queries.reshape(ROWS, HD), tangent_keys.reshape(TOK, HD),
            tangent_values.reshape(TOK, HD), doc_start, out_gain.reshape(1, 512),
        )
        dq, dk, dv = pl.pallas_call(
            hand_on,
            name="hand_on",
            out_shape=tuple(jax.ShapeDtypeStruct(x.shape, F32) for x in (dq, dk, dv)),
            in_specs=[any_space] * 3,
            out_specs=(any_space,) * 3,
            scratch_shapes=[pltpu.VMEM(x.shape, F32) for x in (dq, dk, dv)] + [sems((2, 6))],
        )(dq, dk, dv)
        return dq.reshape(TOK, 4, HD), dk.reshape(TOK, 1, HD), dv.reshape(TOK, 1, HD)

    wide = P("ctx", "head", None)
    return jax.shard_map(
        body,
        mesh=mesh,
        in_specs=(wide, wide, wide, wide, wide, wide, P("ctx"), P("head")),
        out_specs=(wide, wide, wide),
        check_vma=False,
    )
```
